512 devices in a mesh: pencil: 128 (over y, z, core), lev: 4 (over x).
Axes of the slice: x: 4, y: 8, z: 8, core: 2. Of those that a mesh axis runs over, the one named last changes fastest.
Arguments:
- background_std: float32 [4, 4096, 2048], P('lev', 'pencil'), may hold values from 0.4 to 6.1
- x_kernel: float32 [4, 31], P('lev'), may hold values from -0.06 to 0.12
- y_kernel: float32 [4, 31], P('lev'), may hold values from -0.06 to 0.12
- obs_owner: int32 [131072, 1], P(('pencil', 'lev')), may hold values from 0 to 127; in each aligned block of 256 rows (0 to 255, 256 to 511, ...) at most 4 rows name the same one
- obs_cells: int32 [131072, 16], P(('pencil', 'lev')), may hold values from 0 to 65535, as said below
- obs_weights: float32 [131072, 16], P(('pencil', 'lev')), may hold values from -0.05 to 0.2
- innovation: float32 [131072], P(('pencil', 'lev')), may hold values from -6 to 6
- obs_precision: float32 [131072], P(('pencil', 'lev')), may hold values from 0.25 to 4
- obs_counts: int32 [512], P(('pencil', 'lev')), may hold values from 129 to 256, as said below
Outputs:
- control: float32 [4, 2048, 4096], P('lev', 'pencil')
- increment: float32 [4, 4096, 2048], P('lev', 'pencil')
The draws below stay inside these ranges and needn't reach their ends.
Inputs may be any that keep to these rules, and one draw needn't show every extreme that they name: `obs_owner`: no device holds more than 4 observations of one owner, and some device reaches 4. `obs_cells`: indices into the owner's tile of 1 slabs by 32 columns by 2048 rows, flattened in that order. `obs_counts`: some device has all 256 slots live.
All inputs are finite; a program needn't handle non-finite values.
Results may differ from the reference program's by a relative error of at most 0.0001.
Values sent between devices are 32-bit elements; how exact they have to be, the bound alone decides.
A program may use at most 64 MiB of HBM per device.

```python
import math
import jax
import jax.numpy as jnp
import numpy as np

NX = 4096
NY = 2048
KW = 31
ITERS = 2
SLAB_DEV = 1
OBS_DEV = 256
SLABS = 4
TILE_X = 32
CAP = 4
OBS_TOT = 131072
DEVICES_ALL = 512
N_PENCIL = 128
N_LEV = 4


def draw_background_std(key, part):
    latitude = 1.0 + 2.0 * jnp.arange(NY, dtype=jnp.float32) / (NY - 1)
    rough = jnp.exp(jax.random.uniform(key, (SLABS, NX, NY), jnp.float32, -0.7, 0.7))
    return rough * latitude[None, None, :]


def draw_obs_cells(key, part):
    keys = jax.random.split(key, 5)
    slab_pick = jax.random.randint(keys[0], (OBS_TOT, 1), 0, SLAB_DEV)
    anchor_col = jax.random.randint(keys[1], (OBS_TOT, 1), 0, TILE_X)
    anchor_row = jax.random.randint(keys[2], (OBS_TOT, 1), 0, NY)
    offset_col = jax.random.randint(keys[3], (OBS_TOT, 16), 0, 4)
    offset_row = jax.random.randint(keys[4], (OBS_TOT, 16), 0, 4)
    column = (anchor_col + offset_col) % TILE_X
    row_pick = (anchor_row + offset_row) % NY
    return (slab_pick * TILE_X * NY + column * NY + row_pick).astype(jnp.int32)


def draw_obs_counts(key, part):
    first, second = jax.random.split(key)
    base_count = OBS_DEV - jax.random.randint(first, (DEVICES_ALL,), 0, OBS_DEV // 2)
    chosen = jax.random.randint(second, (), 0, DEVICES_ALL)
    return jnp.where(jnp.arange(DEVICES_ALL) == chosen, OBS_DEV, base_count).astype(jnp.int32)


def shard_levels(stream_key, dims, cuts, low, top_value):
    def one(dim, blocks):
        heights = jax.random.uniform(jax.random.fold_in(jax.random.fold_in(stream_key, 6), dim), (blocks,), jnp.float32, low / len(cuts), top_value / len(cuts))
        return jnp.repeat(jnp.exp(heights), dims[dim] // blocks).reshape((-1,) + (1,) * (len(dims) - dim - 1))

    gain = one(*cuts[0])
    for cut in cuts[1:]:
        gain = gain * one(*cut)
    return gain


def assign_block(key, own, number, rows, amount, top, most, slope):
    sequence = jax.random.permutation(key, amount)
    heavy_load, ordinary = shares(amount, rows * top, most, slope, True), shares(amount, rows * top, most, slope, False)
    places = jnp.arange(amount)

    def named(sizes, offset_by):
        used = int((sizes > 0).sum())
        fixed = max(1, used // 4)
        shifted = fixed + (places - fixed + offset_by * (used - fixed)) % max(1, amount - fixed)
        return jnp.zeros((amount,), jnp.int32).at[sequence[jnp.where(places < fixed, places, shifted)]].set(jnp.asarray(sizes, jnp.int32))

    sizes = jnp.where(number % 4 == 0, named(heavy_load, number // 4), named(ordinary, number - number // 4 - 1))
    mixed = jax.random.permutation(jax.random.fold_in(own, 3), amount)
    giver, sink = mixed[0:amount // 2 * 2:2], mixed[1:amount // 2 * 2:2]
    slack = jnp.minimum(sizes[giver] - 1, most - sizes[sink]) // 2
    slack = jnp.where((giver == sequence[0]) | (sink == sequence[0]) | (sizes[sink] == 0), 0, jnp.maximum(slack, 0))
    shifted = jax.random.randint(jax.random.fold_in(own, 4), (amount // 2,), 0, 1 << 20) % (slack + 1)
    sizes = sizes.at[giver].add(-shifted).at[sink].add(shifted)
    labels = jnp.searchsorted(jnp.cumsum(sizes), jnp.arange(rows * top), side="right").astype(jnp.int32)
    grid = labels.reshape(top, rows).T
    grid = grid[jax.random.permutation(jax.random.fold_in(own, 1), rows)]
    offset_by = jax.random.randint(jax.random.fold_in(own, 2), (rows, 1), 0, top)
    return jnp.take_along_axis(grid, (jnp.arange(top)[None, :] + offset_by) % top, axis=1)


def shares(number_of, total, most, lean, full):
    portions = [(1 << 20) // math.isqrt(rank ** lean) + 1 for rank in range(1, number_of + 1)]
    largest = most if full else min(most, max(-(-total // number_of), total * portions[0] // sum(portions)))
    least = 1 if total - largest >= number_of - 1 else 0
    counts, surplus = [largest] + [least] * (number_of - 1), total - largest - least * (number_of - 1)
    while surplus > 0:
        candidates = [i for i in range(1, number_of) if counts[i] < largest] or [i for i in range(1, number_of) if counts[i] < most]
        mass, remaining = sum([portions[i] for i in candidates]), surplus
        for i in candidates:
            more = min(most - counts[i], max(1, remaining * portions[i] // mass), surplus)
            counts[i] = counts[i] + more
            surplus = surplus - more
    return np.array(counts)


def bell_draw(stream_key, extent, width, limit, cuts=(), held_as=jnp.bfloat16):
    values = jax.random.normal(stream_key, extent, jnp.float32) * width
    if len(cuts) > 0:
        values = shard_levels(stream_key, extent, cuts, -0.22, 0.18) * values
    return jnp.clip(values, min=-limit, max=limit).astype(held_as)


def setup_inputs(seed: int = 0) -> dict:
    key_of = jax.random.split(jax.random.key(seed), 10)
    background_std = draw_background_std(jax.random.fold_in(key_of[9], 71), 0)
    x_kernel = jnp.clip(-0.06 + 0.179999996 * jax.random.uniform(key_of[1], (SLABS, KW), jnp.float32) ** shard_levels(key_of[1], (SLABS, KW), ((0, 4),), -0.2, 0.2), -0.06, 0.12)
    y_kernel = jnp.clip(-0.06 + 0.179999996 * jax.random.uniform(key_of[2], (SLABS, KW), jnp.float32) ** shard_levels(key_of[2], (SLABS, KW), ((0, 4),), -0.2, 0.2), -0.06, 0.12)
    obs_owner_keys = jax.random.split(jax.random.fold_in(key_of[3], 1), OBS_TOT // OBS_DEV)
    obs_owner_turns = jax.random.permutation(jax.random.fold_in(key_of[3], 3), OBS_TOT // OBS_DEV)
    obs_owner = jax.vmap(lambda own, number: assign_block(jax.random.fold_in(key_of[3], 2), own, number, OBS_DEV, N_PENCIL, 1, CAP, 2))(obs_owner_keys, obs_owner_turns).reshape((OBS_TOT, 1))
    obs_cells = draw_obs_cells(jax.random.fold_in(key_of[9], 71), 0)
    obs_weights = jnp.clip(-0.05 + 0.25 * jax.random.uniform(key_of[5], (OBS_TOT, 16), jnp.float32) ** shard_levels(key_of[5], (OBS_TOT, 16), ((0, 512),), -0.2, 0.2), -0.05, 0.2)
    innovation = bell_draw(key_of[6], (OBS_TOT,), 1.0, 6.0, ((0, 512),), jnp.float32)
    obs_precision = jnp.clip(jnp.exp(math.log(4.0) - 2.7725887 * jax.random.uniform(key_of[7], (OBS_TOT,), jnp.float32) ** shard_levels(key_of[7], (OBS_TOT,), ((0, 512),), -0.2, 0.2)), 0.25, 4.0)
    obs_counts = draw_obs_counts(jax.random.fold_in(key_of[9], 71), 0)
    return dict(background_std=background_std, x_kernel=x_kernel, y_kernel=y_kernel, obs_owner=obs_owner, obs_cells=obs_cells, obs_weights=obs_weights, innovation=innovation, obs_precision=obs_precision, obs_counts=obs_counts)


def smooth(grid_field, kernel_taps, periodic):
    taps = kernel_taps.shape[1]
    margin = taps // 2
    length = grid_field.shape[2]
    if periodic:
        padded = jnp.concatenate([grid_field[:, :, length - margin:], grid_field, grid_field[:, :, :margin]], axis=2)
    else:
        padded = jnp.pad(grid_field, ((0, 0), (0, 0), (margin, margin)))
    result = jnp.zeros(grid_field.shape, jnp.float32)
    for offset in range(taps):
        result = result + kernel_taps[:, offset][:, None, None] * padded[:, :, offset:offset + length]
    return result


def reference(background_std, x_kernel, y_kernel, obs_owner, obs_cells, obs_weights, innovation, obs_precision, obs_counts):
    tile_cols = NX // N_PENCIL
    ordinal = jnp.arange(OBS_TOT, dtype=jnp.int32)
    holder = ordinal // OBS_DEV
    group = (holder % N_LEV)[:, None]
    living = ((ordinal % OBS_DEV) < obs_counts[holder]).astype(jnp.float32)
    slab_index = group * SLAB_DEV + obs_cells // (tile_cols * NY)
    column = obs_owner[:, 0:1] * tile_cols + (obs_cells // NY) % tile_cols
    flat_index = ((slab_index * NX + column) * NY + obs_cells % NY).astype(jnp.int32)
    weight = obs_precision * living

    def forward(grid_field):
        along_x = smooth(grid_field, x_kernel, True)
        return background_std * smooth(jnp.swapaxes(along_x, 1, 2), y_kernel, False)

    def adjoint(grid_field):
        along_y = smooth(background_std * grid_field, y_kernel[:, ::-1], False)
        return smooth(jnp.swapaxes(along_y, 1, 2), x_kernel[:, ::-1], True)

    def observe(grid_field):
        return jnp.sum(obs_weights * grid_field.reshape(-1)[flat_index], axis=1)

    def spread(values):
        total = jnp.zeros((SLABS * NX * NY,), jnp.float32)
        total = total.at[flat_index.reshape(-1)].add((obs_weights * values[:, None]).reshape(-1))
        return total.reshape(SLABS, NX, NY)

    gradient_rhs = adjoint(spread(weight * innovation))
    control = jnp.zeros_like(gradient_rhs)
    resid = gradient_rhs
    direction = gradient_rhs
    norm_now = jnp.sum(resid * resid)
    for iteration in range(ITERS):
        image = direction + adjoint(spread(weight * observe(forward(direction))))
        step_length = norm_now / jnp.sum(direction * image)
        control = control + step_length * direction
        resid = resid - step_length * image
        norm_next = jnp.sum(resid * resid)
        direction = resid + (norm_next / norm_now) * direction
        norm_now = norm_next
    return control, forward(control)
```

```python
import functools

import jax
import jax.numpy as jnp
from jax import lax
from jax.experimental import pallas as pl
from jax.experimental.pallas import tpu as pltpu
from jax.sharding import PartitionSpec as P

F32, BF16, I32 = jnp.float32, jnp.bfloat16, jnp.int32
MESH = pl.DeviceIdType.MESH
HALF = 15
PENCILS = 128
LEVS = 4
NEAR = 16
FAR_Y = 8
SLOTS = 4
NT = (((1,), (1,)), ((), ()))


def dot(a, b):
    return jnp.dot(a, b, preferred_element_type=F32)


def pieces(v):
    hi = v.astype(BF16)
    return hi, (v - hi.astype(F32)).astype(BF16)


def band(delta, taps, sign):
    out = jnp.zeros(delta.shape, F32)
    for d in range(-HALF, HALF + 1):
        out = jnp.where(delta == d, taps[0, HALF + sign * d], out)
    return out


def lane_blocks(x):
    lane = lax.broadcasted_iota(I32, x[0].shape, x[0].ndim - 1)
    ax = x[0].ndim - 1
    low, even = lane < 64, (lane & 32) == 0

    def halves(a, b):
        return jnp.where(low, a, pltpu.roll(b, 64, ax)), jnp.where(low, pltpu.roll(a, 64, ax), b)

    def quarters(a, b):
        return jnp.where(even, a, pltpu.roll(b, 32, ax)), jnp.where(even, pltpu.roll(a, 96, ax), b)

    a, c = halves(x[0], x[2])
    b, d = halves(x[1], x[3])
    return quarters(a, b) + quarters(c, d)


def kernel(
    std_in, xk, yk, owner, cells, weights, innov, prec, counts,
    control_out, incr_out,
    osend, orecv, rt_ref, hi_ref, lo_ref, w_ref, lot,
    ty, tyt, ax_ref, std, g2, acc,
    fown, fl, fr, vbuf, bbuf, ubuf, bb_f, bu_f,
    xsend, xrecv, asend, arecv, csend, crecv,
    osem, hsem_s, hsem_r, xsem, asem, csem, lsem,
):
    me = lax.axis_index("pencil")
    lev = lax.axis_index("lev")
    near = lax.rem(me, NEAR)
    row = lax.div(me, NEAR)
    left, right = lax.rem(me + PENCILS - 1, PENCILS), lax.rem(me + 1, PENCILS)

    barrier = pltpu.get_barrier_semaphore()

    @pl.loop(1, PENCILS)
    def _(i):
        pl.semaphore_signal(barrier, inc=1, device_id=(lax.rem(me + i, PENCILS), lev), device_id_type=MESH)

    @pl.loop(FAR_Y, FAR_Y * LEVS)
    def _(i):
        pl.semaphore_signal(
            barrier,
            inc=1,
            device_id=(lax.rem(row + i, FAR_Y) * NEAR + near, lax.rem(lev + lax.div(i, FAR_Y), LEVS)),
            device_id_type=MESH,
        )

    n_obs = cells.shape[1]
    lane_o = lax.broadcasted_iota(I32, (1, n_obs), 1)
    weight = jnp.where(lane_o < counts[0], prec[...], 0.0)
    member = lax.broadcasted_iota(I32, (PENCILS, n_obs), 0) == owner[...]
    member_b = jnp.where(member, 1.0, 0.0).astype(BF16)
    before = lax.broadcasted_iota(I32, (n_obs, n_obs), 0) < lax.broadcasted_iota(I32, (n_obs, n_obs), 1)
    rank = dot(member_b, jnp.where(before, 1.0, 0.0).astype(BF16))
    sub8 = lax.broadcasted_iota(I32, (8, n_obs), 0)
    tail = jnp.where(sub8 == 0, weight * innov[...], jnp.where(sub8 == 1, weight, 0.0))
    feats = jnp.concatenate(
        [cells[...].astype(F32), weights[...], tail, jnp.zeros((24, n_obs), F32)], axis=0
    )
    f0 = feats.astype(BF16)
    rest = feats - f0.astype(F32)
    f1 = rest.astype(BF16)
    f2 = (rest - f1.astype(F32)).astype(BF16)
    packed = []
    for s in range(SLOTS):
        pick = jnp.where(member, jnp.where(rank == float(s), 1.0, 0.0), 0.0).astype(BF16)
        parts = [lax.dot_general(pick, f, NT, preferred_element_type=F32) for f in (f0, f1, f2)]
        packed.append(parts[0] + parts[1] + parts[2])
    for h in range(2):
        osend[pl.ds(h, PENCILS, stride=2), :] = jnp.concatenate(packed[2 * h : 2 * h + 2], axis=1)

    pl.semaphore_wait(barrier, PENCILS - 1 + FAR_Y * (LEVS - 1))

    own = pltpu.make_async_copy(osend.at[pl.ds(me * 2, 2)], orecv.at[pl.ds(me * 2, 2)], lsem.at[0])
    own.start()

    def obs_copy(q, n=1):
        return pltpu.make_async_remote_copy(
            src_ref=osend.at[pl.ds(q * 2, 2 * n)],
            dst_ref=orecv.at[pl.ds((me if n == 1 else 0) * 2, 2 * n)],
            send_sem=osem.at[0],
            recv_sem=osem.at[1],
            device_id=(q if n == 1 else right, lev),
            device_id_type=MESH,
        )

    @pl.loop(1, PENCILS)
    def _(i):
        obs_copy(lax.rem(me + i, PENCILS)).start()

    base_delta = lax.broadcasted_iota(I32, (8, 512), 0) - lax.broadcasted_iota(I32, (8, 512), 1) + 256
    for sign, ref in ((1, ty), (-1, tyt)):
        base = band(base_delta, yk, sign)
        for g in range(48):
            p0 = 8 * g if g < 40 else 8 * g - 384
            r = pltpu.roll(base, (p0 - 256) % 512, 1)[:, :256]
            acc[8 * g : 8 * g + 8, :] = r
        hi, lo = pieces(acc[0:384, :])
        ref[0:384, :] = hi
        ref[384:768, :] = lo
    delta = lax.broadcasted_iota(I32, (32, 96), 1) - lax.broadcasted_iota(I32, (32, 96), 0) - 32
    delta_w = lax.broadcasted_iota(I32, (96, 96), 1) - lax.broadcasted_iota(I32, (96, 96), 0)
    a1 = band(delta, xk, -1)
    a2 = jnp.dot(
        band(delta, xk, 1),
        band(delta_w, xk, -1),
        preferred_element_type=F32,
        precision=lax.Precision.HIGHEST,
    )
    a_hi, a_lo = pieces(jnp.concatenate([a1, a2], axis=0))
    ax_ref[0:64, :] = a_hi
    ax_ref[64:128, :] = a_lo
    for t in range(8):
        std[t * 32 : t * 32 + 32, :] = std_in[0, :, t * 256 : t * 256 + 256]

    own.wait()
    everyone = obs_copy(0, PENCILS - 1)
    everyone.wait_send()
    everyone.wait_recv()

    for h in range(2):
        rt_ref[h * 128 : h * 128 + 128, :] = orecv[pl.ds(h, PENCILS, stride=2), :].T
    wd, wgt = [], []
    for s in range(SLOTS):
        c = rt_ref[s * 64 : s * 64 + 16, :].astype(I32)
        cols = slice(s * 128, s * 128 + 128)
        hi_ref[:, cols] = (((c >> 8) & 7) * 32 + (c >> 11)).astype(F32)
        lo_ref[:, cols] = (c & 255).astype(F32)
        w_ref[:, cols] = rt_ref[s * 64 + 16 : s * 64 + 32, :]
        wd.append(rt_ref[s * 64 + 32 : s * 64 + 33, :])
        wgt.append(rt_ref[s * 64 + 33 : s * 64 + 34, :])
    wd, wgt = jnp.concatenate(wd, axis=1), jnp.concatenate(wgt, axis=1)
    iota_f = lax.broadcasted_iota(I32, (256, 128), 0).astype(F32)
    iota_b = iota_f.astype(BF16)
    iota_b4 = jnp.concatenate([iota_b] * 4, axis=1)
    iota_f4 = jnp.concatenate([iota_f] * 4, axis=1)

    @pl.loop(0, 16)
    def _(k):
        lo = lo_ref[pl.ds(k, 1), :].astype(BF16)
        lot[k] = jnp.where(iota_b4 == lo, jnp.bfloat16(1), jnp.bfloat16(0))

    def spread(z):
        acc[...] = jnp.zeros_like(acc)

        @pl.loop(0, 16)
        def _(k):
            hit = iota_b4 == hi_ref[pl.ds(k, 1), :].astype(BF16)
            z_hi, z_lo = pieces(w_ref[pl.ds(k, 1), :] * z)
            zero = jnp.bfloat16(0)
            lhs = jnp.concatenate([jnp.where(hit, z_hi, zero), jnp.where(hit, z_lo, zero)], axis=0)
            acc[...] += lax.dot_general(lhs, lot[k], NT, preferred_element_type=F32)

        return acc[0:256, :] + acc[256:512, :]

    def observe(field):
        g_hi, g_lo = pieces(field)
        g2[0:256, :] = g_hi
        g2[256:512, :] = g_lo

        def step(k, total):
            t = dot(g2[...], lot[k])
            hit = iota_f4 == hi_ref[pl.ds(k, 1), :]
            found = jnp.where(hit, t[0:256] + t[256:512], 0.0)
            return total + w_ref[pl.ds(k, 1), :] * jnp.sum(found.reshape(32, 8, 512), axis=0)

        total = lax.fori_loop(0, 16, step, jnp.zeros((8, 512), F32))
        return jnp.sum(total, axis=0, keepdims=True)

    edge_low = lax.broadcasted_iota(I32, (256, 128), 1) < 64

    def along_y(g, ref):
        blank = jnp.zeros((32, 128), F32)
        up = jnp.concatenate([g[32:, 0:128], blank], axis=0)
        down = jnp.concatenate([blank, g[:224, 128:256]], axis=0)
        full = jnp.concatenate([g, jnp.where(edge_low, up, down)], axis=1)
        hi, lo = pieces(full)
        t_hi, t_lo = ref[0:384, :], ref[384:768, :]
        return dot(hi, t_hi) + dot(lo, t_hi) + dot(hi, t_lo)

    def halo(n, z):
        fown[n] = along_y(std[...] * spread(z), tyt)
        both = []
        for side, (to, dst) in enumerate(((left, fr), (right, fl))):
            both.append(
                pltpu.make_async_remote_copy(
                    src_ref=fown.at[n],
                    dst_ref=dst.at[n],
                    send_sem=hsem_s.at[n, side],
                    recv_sem=hsem_r.at[n, side],
                    device_id=(to, lev),
                    device_id_type=MESH,
                )
            )
            both[-1].start()
        for copy in both:
            copy.wait()

    def along_x(n, out):
        for t in range(8):
            rows = slice(t * 32, t * 32 + 32)
            window = jnp.concatenate([fl[n, rows, :], fown[n, rows, :], fr[n, rows, :]], axis=0)
            hi, lo = pieces(window)
            r1 = dot(ax_ref[...], hi)
            r = r1[0:64] + r1[64:128] + dot(ax_ref[0:64, :], lo)
            out[rows, :] = r[0:32]
            vbuf[rows, :] = r[32:64]

    halo(0, wd)
    along_x(0, bbuf)
    bb_f[...] = std[...] * along_y(vbuf[...], ty)
    y0 = observe(bb_f[...])
    halo(1, wgt * y0)
    along_x(1, ubuf)

    for g in range(2):
        for h in range(2):
            x = []
            for buf in (bbuf, ubuf):
                turned = buf[g * 128 : g * 128 + 128, h * 128 : h * 128 + 128].T
                turned = turned.reshape(8, 16, 128)
                x += [turned[:, 0:8, :], turned[:, 8:16, :]]
            for t, m in enumerate(lane_blocks(x)):
                at = ((4 * g + t) * 16 + h * 8) * 8
                xsend[at : at + 64, :] = m.reshape(64, 128)

    own2 = pltpu.make_async_copy(xsend.at[pl.ds(me * 8, 8)], xrecv.at[pl.ds(me * 8, 8)], lsem.at[1])
    own2.start()

    def turn_copy(q, n=1):
        return pltpu.make_async_remote_copy(
            src_ref=xsend.at[pl.ds(q * 8, 8 * n)],
            dst_ref=xrecv.at[pl.ds((me if n == 1 else 0) * 8, 8 * n)],
            send_sem=xsem.at[0],
            recv_sem=xsem.at[1],
            device_id=(q if n == 1 else right, lev),
            device_id_type=MESH,
        )

    @pl.loop(1, PENCILS)
    def _(i):
        turn_copy(lax.rem(me + i, PENCILS)).start()

    bu_f[...] = std[...] * along_y(vbuf[...], ty)
    y1 = observe(bu_f[...])

    def fold(v):
        return jnp.sum(v.reshape(32, 8, 256), axis=0)

    def cells_row(p):
        p = fold(p)
        return jnp.sum(p[:, 0:128] + p[:, 128:256], axis=0, keepdims=True)

    def obs_row(p):
        return p[:, 0:128] + p[:, 128:256] + p[:, 256:384] + p[:, 384:512]

    b, u = bbuf[...], ubuf[...]
    rows6 = [
        cells_row(b * b), cells_row(b * u), cells_row(u * u),
        obs_row(wgt * y0 * y0), obs_row(wgt * y0 * y1), obs_row(wgt * y1 * y1),
    ]
    sub = lax.broadcasted_iota(I32, (8, 128), 0)
    stack = jnp.zeros((8, 128), F32)
    for i, r in enumerate(rows6):
        stack = jnp.where(sub == i, r, stack)
    sums = jnp.sum(stack, axis=1, keepdims=True)
    diagonal = sub == lax.broadcasted_iota(I32, (8, 128), 1)
    local = jnp.sum(jnp.where(diagonal, sums, 0.0), axis=0, keepdims=True)

    def sum_over(mine, n, count, send, recv, sem, target):
        send[0] = mine
        recv[n] = mine

        def copy(i, many=False):
            return pltpu.make_async_remote_copy(
                src_ref=recv.at[pl.ds(0, count - 1)] if many else send.at[pl.ds(0, 1)],
                dst_ref=recv.at[pl.ds(0, count - 1)] if many else recv.at[pl.ds(n, 1)],
                send_sem=sem.at[0],
                recv_sem=sem.at[1],
                device_id=target(i),
                device_id_type=MESH,
            )

        @pl.loop(1, count)
        def _(i):
            copy(lax.rem(n + i, count)).start()

        done = copy(0, True)
        done.wait_send()
        done.wait_recv()
        total = recv[0]
        for i in range(1, count):
            total = total + recv[i]
        return total

    total = sum_over(local, near, NEAR, asend, arecv, asem, lambda i: (row * NEAR + i, lev))
    total = sum_over(
        total, row * LEVS + lev, FAR_Y * LEVS, csend, crecv, csem,
        lambda i: (lax.div(i, LEVS) * NEAR + near, lax.rem(i, LEVS)),
    )
    bb, bu, uu, q00, q01, q11 = [total[:, i : i + 1] for i in range(6)]

    ratio = bu / bb
    alpha0 = 1.0 / (1.0 + ratio)
    norm1 = alpha0 * alpha0 * (uu - ratio * bu)
    gb = ratio * alpha0 + norm1 / bb
    gu = -alpha0
    curve = gb * gb * (bb + q00) + 2.0 * gb * gu * (bu + q01) + gu * gu * (uu + q11)
    alpha1 = norm1 / curve
    c_b = alpha0 + alpha1 * gb
    c_u = alpha1 * gu

    for t in range(8):
        rows = slice(t * 32, t * 32 + 32)
        incr_out[0, :, t * 256 : t * 256 + 256] = c_b * bb_f[rows, :] + c_u * bu_f[rows, :]

    own2.wait()
    turned = turn_copy(0, PENCILS - 1)
    turned.wait_send()
    turned.wait_recv()
    got = xrecv[...].reshape(32, 4, 8, 128)
    parts = lane_blocks([got[:, i] for i in range(4)])
    for rh in range(2):
        value = c_b * parts[rh] + c_u * parts[2 + rh]
        for p in range(32):
            control_out[0, rh * 8 : rh * 8 + 8, p * 128 : p * 128 + 128] = value[p]


def body(background_std, x_kernel, y_kernel, obs_owner, obs_cells, obs_weights, innovation, obs_precision, obs_counts):
    holding = obs_owner.shape[0]
    vmem = pl.BlockSpec(memory_space=pltpu.VMEM)
    smem = pl.BlockSpec(memory_space=pltpu.SMEM)
    field = pltpu.VMEM((256, 256), F32)
    dma = pltpu.SemaphoreType.DMA
    return pl.pallas_call(
        kernel,
        out_shape=(
            jax.ShapeDtypeStruct((1, 16, 4096), F32),
            jax.ShapeDtypeStruct((1, 32, 2048), F32),
        ),
        in_specs=[vmem, smem, smem, vmem, vmem, vmem, vmem, vmem, smem],
        out_specs=(vmem, vmem),
        scratch_shapes=[
            pltpu.VMEM((256, 128), F32), pltpu.VMEM((256, 128), F32),
            pltpu.VMEM((256, 128), F32),
            pltpu.VMEM((16, 512), F32), pltpu.VMEM((16, 512), F32), pltpu.VMEM((16, 512), F32),
            pltpu.VMEM((16, 256, 512), BF16),
            pltpu.VMEM((768, 256), BF16), pltpu.VMEM((768, 256), BF16),
            pltpu.VMEM((128, 96), BF16),
            field,
            pltpu.VMEM((512, 256), BF16),
            pltpu.VMEM((512, 256), F32),
            pltpu.VMEM((2, 256, 256), F32), pltpu.VMEM((2, 256, 256), F32), pltpu.VMEM((2, 256, 256), F32),
            field, field, field, field, field,
            pltpu.VMEM((1024, 128), F32), pltpu.VMEM((1024, 128), F32),
            pltpu.VMEM((1, 1, 128), F32), pltpu.VMEM((NEAR, 1, 128), F32),
            pltpu.VMEM((1, 1, 128), F32), pltpu.VMEM((FAR_Y * LEVS, 1, 128), F32),
            dma((2,)), dma((2, 2)), dma((2, 2)), dma((2,)), dma((2,)), dma((2,)), dma((2,)),
        ],
        compiler_params=pltpu.CompilerParams(
            collective_id=0, has_side_effects=True, vmem_limit_bytes=48 << 20
        ),
        name="assimilate",
    )(
        background_std, x_kernel, y_kernel, obs_owner.reshape(1, holding), obs_cells.T, obs_weights.T,
        innovation.reshape(1, holding), obs_precision.reshape(1, holding), obs_counts,
    )


def solution(mesh):
    return jax.shard_map(
        body,
        mesh=mesh,
        in_specs=(
            P("lev", "pencil", None),
            P("lev", None),
            P("lev", None),
            P(("pencil", "lev"), None),
            P(("pencil", "lev"), None),
            P(("pencil", "lev"), None),
            P(("pencil", "lev")),
            P(("pencil", "lev")),
            P(("pencil", "lev")),
        ),
        out_specs=(P("lev", "pencil", None), P("lev", "pencil", None)),
        check_vma=False,
    )
```

```python
import functools

import jax
import jax.numpy as jnp
from jax import lax
from jax.experimental import pallas as pl
from jax.experimental.pallas import tpu as pltpu
from jax.sharding import PartitionSpec as P

F32, BF16, I32 = jnp.float32, jnp.bfloat16, jnp.int32
MESH = pl.DeviceIdType.MESH
HALF = 15
PENCILS = 128
LEVS = 4
NEAR = 16
FAR_Y = 8
SLOTS = 4
NT = (((1,), (1,)), ((), ()))
FARTHEST = (8, 7, 9, 6, 10, 5, 11, 4, 12, 3, 13, 2, 14, 1, 15, 0)
CHUNKS = 2
PART = 256 // CHUNKS


def dot(a, b):
    return jnp.dot(a, b, preferred_element_type=F32)


def pieces(v):
    hi = v.astype(BF16)
    return hi, (v - hi.astype(F32)).astype(BF16)


def band(delta, taps, sign):
    out = jnp.zeros(delta.shape, F32)
    for d in range(-HALF, HALF + 1):
        out = jnp.where(delta == d, taps[0, HALF + sign * d], out)
    return out


def lane_blocks(x):
    lane = lax.broadcasted_iota(I32, x[0].shape, x[0].ndim - 1)
    ax = x[0].ndim - 1
    low, even = lane < 64, (lane & 32) == 0

    def halves(a, b):
        return jnp.where(low, a, pltpu.roll(b, 64, ax)), jnp.where(low, pltpu.roll(a, 64, ax), b)

    def quarters(a, b):
        return jnp.where(even, a, pltpu.roll(b, 32, ax)), jnp.where(even, pltpu.roll(a, 96, ax), b)

    a, c = halves(x[0], x[2])
    b, d = halves(x[1], x[3])
    return quarters(a, b) + quarters(c, d)


def kernel(
    std_hbm, xk_hbm, yk_hbm, owner_hbm, cells_hbm, weights_hbm, innov_hbm, prec_hbm, counts_hbm,
    control_out, incr_out,
    std_in, xk, yk, owner, cells, weights, innov, prec, counts,
    osend, orecv, rt_ref, hi_ref, lo_ref, w_ref, lot,
    ty, tyt, ax_ref, std, g2, acc,
    fown, fl, fr, vbuf, bbuf, ubuf, bb_f, bu_f,
    turned, ctl, xsend, xrecv, asend, arecv, csend, crecv,
    isem, osem, hsem_s, hsem_r, xsem, asem, csem, lsem,
):
    me = lax.axis_index("pencil")
    lev = lax.axis_index("lev")
    near = lax.rem(me, NEAR)
    row = lax.div(me, NEAR)
    left, right = lax.rem(me + PENCILS - 1, PENCILS), lax.rem(me + 1, PENCILS)
    zcs = [lax.rem(near + j, NEAR) for j in FARTHEST]

    def peer_row(i):
        dy = FAR_Y // 2 + lax.div(i + 1, 2) * (1 - 2 * lax.rem(i, 2))
        return lax.rem(row + dy, FAR_Y) * NEAR

    def each_peer(act):
        @pl.loop(0, FAR_Y - 1)
        def _(i):
            base = peer_row(i)
            for zc in zcs:
                act(base + zc)

        for zc in zcs[:-1]:
            act(row * NEAR + zc)

    loads = [
        pltpu.make_async_copy(src, dst, isem.at[i])
        for i, (src, dst) in enumerate(
            (
                (owner_hbm, owner), (prec_hbm, prec), (innov_hbm, innov), (counts_hbm, counts),
                (cells_hbm, cells), (weights_hbm, weights), (xk_hbm, xk), (yk_hbm, yk), (std_hbm, std_in),
            )
        )
    ]
    for load in loads:
        load.start()
    barrier = pltpu.get_barrier_semaphore()

    def hello(q, to_lev=lev):
        pl.semaphore_signal(barrier, inc=1, device_id=(q, to_lev), device_id_type=MESH)

    each_peer(hello)

    @pl.loop(0, FAR_Y)
    def _(i):
        for dx in (2, 1, 3):
            hello(lax.rem(row + FAR_Y // 2 + i, FAR_Y) * NEAR + near, lax.rem(lev + dx, LEVS))

    for load in loads[:6]:
        load.wait()

    n_obs = cells.shape[1]
    lane_o = lax.broadcasted_iota(I32, (1, n_obs), 1)
    weight = jnp.where(lane_o < counts[0, 0], prec[...], 0.0)
    member = lax.broadcasted_iota(I32, (PENCILS, n_obs), 0) == owner[...]
    member_b = jnp.where(member, 1.0, 0.0).astype(BF16)
    before = lax.broadcasted_iota(I32, (n_obs, n_obs), 0) < lax.broadcasted_iota(I32, (n_obs, n_obs), 1)
    rank = dot(member_b, jnp.where(before, 1.0, 0.0).astype(BF16))
    sub8 = lax.broadcasted_iota(I32, (8, n_obs), 0)
    tail = jnp.where(sub8 == 0, weight * innov[...], jnp.where(sub8 == 1, weight, 0.0))
    feats = jnp.concatenate(
        [cells[...].astype(F32), weights[...], tail, jnp.zeros((24, n_obs), F32)], axis=0
    )
    f0 = feats.astype(BF16)
    rest = feats - f0.astype(F32)
    f1 = rest.astype(BF16)
    f2 = (rest - f1.astype(F32)).astype(BF16)
    packed = []
    for s in range(SLOTS):
        pick = jnp.where(member, jnp.where(rank == float(s), 1.0, 0.0), 0.0).astype(BF16)
        parts = [lax.dot_general(pick, f, NT, preferred_element_type=F32) for f in (f0, f1, f2)]
        packed.append(parts[0] + parts[1] + parts[2])
    for h in range(2):
        osend[pl.ds(h, PENCILS, stride=2), :] = jnp.concatenate(packed[2 * h : 2 * h + 2], axis=1)

    pl.semaphore_wait(barrier, PENCILS - 1 + FAR_Y * (LEVS - 1))

    own = pltpu.make_async_copy(osend.at[pl.ds(me * 2, 2)], orecv.at[pl.ds(me * 2, 2)], lsem.at[0])
    own.start()

    def obs_copy(q, n=1):
        return pltpu.make_async_remote_copy(
            src_ref=osend.at[pl.ds(q * 2, 2 * n)],
            dst_ref=orecv.at[pl.ds((me if n == 1 else 0) * 2, 2 * n)],
            send_sem=osem.at[0],
            recv_sem=osem.at[1],
            device_id=(q if n == 1 else right, lev),
            device_id_type=MESH,
        )

    each_peer(lambda q: obs_copy(q).start())
    for load in loads[6:]:
        load.wait()

    base_delta = lax.broadcasted_iota(I32, (8, 512), 0) - lax.broadcasted_iota(I32, (8, 512), 1) + 256
    for sign, ref in ((1, ty), (-1, tyt)):
        base = band(base_delta, yk, sign)
        for g in range(48):
            p0 = 8 * g if g < 40 else 8 * g - 384
            r = pltpu.roll(base, (p0 - 256) % 512, 1)[:, :256]
            acc[8 * g : 8 * g + 8, :] = r
        hi, lo = pieces(acc[0:384, :])
        ref[0:384, :] = hi
        ref[384:768, :] = hi
        ref[768:1152, :] = lo
    delta = lax.broadcasted_iota(I32, (32, 96), 1) - lax.broadcasted_iota(I32, (32, 96), 0) - 32
    delta_w = lax.broadcasted_iota(I32, (96, 96), 1) - lax.broadcasted_iota(I32, (96, 96), 0)
    a1 = band(delta, xk, -1)
    a2 = jnp.dot(
        band(delta, xk, 1),
        band(delta_w, xk, -1),
        preferred_element_type=F32,
        precision=lax.Precision.HIGHEST,
    )
    a_hi, a_lo = pieces(jnp.concatenate([a1, a2], axis=0))
    ax_ref[0:64, :] = a_hi
    ax_ref[64:128, :] = a_lo
    for t in range(8):
        std[t * 32 : t * 32 + 32, :] = std_in[0, :, t * 256 : t * 256 + 256]

    own.wait()
    everyone = obs_copy(0, PENCILS - 1)
    everyone.wait_send()
    everyone.wait_recv()

    for h in range(2):
        rt_ref[h * 128 : h * 128 + 128, :] = orecv[pl.ds(h, PENCILS, stride=2), :].T
    wd, wgt = [], []
    for s in range(SLOTS):
        c = rt_ref[s * 64 : s * 64 + 16, :].astype(I32)
        cols = slice(s * 128, s * 128 + 128)
        hi_ref[:, cols] = (((c >> 8) & 7) * 32 + (c >> 11)).astype(F32)
        lo_ref[:, cols] = (c & 255).astype(F32)
        w_ref[:, cols] = rt_ref[s * 64 + 16 : s * 64 + 32, :]
        wd.append(rt_ref[s * 64 + 32 : s * 64 + 33, :])
        wgt.append(rt_ref[s * 64 + 33 : s * 64 + 34, :])
    wd, wgt = jnp.concatenate(wd, axis=1), jnp.concatenate(wgt, axis=1)
    iota_f = lax.broadcasted_iota(I32, (256, 128), 0).astype(F32)
    iota_b = iota_f.astype(BF16)
    iota_b4 = jnp.concatenate([iota_b] * 4, axis=1)
    iota_f4 = jnp.concatenate([iota_f] * 4, axis=1)
    one, zero = jnp.bfloat16(1), jnp.bfloat16(0)

    def spread(z, first):
        acc[...] = jnp.zeros_like(acc)

        @pl.loop(0, 4)
        def _(n):
            lhs = []
            for j in range(4):
                k = n * 4 + j
                if first:
                    lo = lo_ref[pl.ds(k, 1), :].astype(BF16)
                    lot[n, :, j * 512 : j * 512 + 512] = jnp.where(iota_b4 == lo, one, zero)
                hit = iota_b4 == hi_ref[pl.ds(k, 1), :].astype(BF16)
                z_hi, z_lo = pieces(w_ref[pl.ds(k, 1), :] * z)
                lhs.append(jnp.concatenate([jnp.where(hit, z_hi, zero), jnp.where(hit, z_lo, zero)], axis=0))
            acc[...] += lax.dot_general(jnp.concatenate(lhs, axis=1), lot[n], NT, preferred_element_type=F32)

        return acc[0:256, :] + acc[256:512, :]

    def observe(field, send):
        g_hi, g_lo = pieces(field)
        g2[0:256, :] = g_hi
        g2[256:512, :] = g_lo
        for i in (1, 3, 5):
            send(peer_row(i) + zcs[-1])

        def step(n, total):
            first, second = peer_row(2 * n), peer_row(2 * n + 1)
            for zc in zcs:
                send(first + zc)
            for zc in zcs[:-1]:
                send(second + zc)
            both = dot(g2[...], lot[n])
            for j in range(4):
                k = n * 4 + j
                t = both[:, j * 512 : j * 512 + 512]
                found = jnp.where(iota_f4 == hi_ref[pl.ds(k, 1), :], t[0:256] + t[256:512], 0.0)
                total += w_ref[pl.ds(k, 1), :] * jnp.sum(found.reshape(32, 8, 512), axis=0)
            return total

        total = lax.fori_loop(0, 4, step, jnp.zeros((8, 512), F32))
        return jnp.sum(total, axis=0, keepdims=True)

    edge_low = lax.broadcasted_iota(I32, (256, 128), 1) < 64

    def y_operand(g):
        blank = jnp.zeros((32, 128), F32)
        up = jnp.concatenate([g[32:, 0:128], blank], axis=0)
        down = jnp.concatenate([blank, g[:224, 128:256]], axis=0)
        hi, lo = pieces(jnp.concatenate([g, jnp.where(edge_low, up, down)], axis=1))
        return jnp.concatenate([hi, lo, hi], axis=1)

    def halo(n, z):
        operand = y_operand(std[...] * spread(z, n == 0))
        copies = []
        for c in range(CHUNKS):
            rows = slice(c * PART, c * PART + PART)
            fown[n, rows, :] = dot(operand[rows], tyt[...])
            both = []
            for side, (to, dst) in enumerate(((left, fr), (right, fl))):
                both.append(
                    pltpu.make_async_remote_copy(
                        src_ref=fown.at[n, pl.ds(c * PART, PART)],
                        dst_ref=dst.at[n, pl.ds(c * PART, PART)],
                        send_sem=hsem_s.at[n, side, c],
                        recv_sem=hsem_r.at[n, side, c],
                        device_id=(to, lev),
                        device_id_type=MESH,
                    )
                )
                both[-1].start()
            copies.append(both)
        return copies

    def along_x(n, copies, out):
        for c in range(CHUNKS):
            for copy in copies[c]:
                copy.wait_recv()
            for t in range(c * 8 // CHUNKS, (c + 1) * 8 // CHUNKS):
                rows = slice(t * 32, t * 32 + 32)
                window = jnp.concatenate([fl[n, rows, :], fown[n, rows, :], fr[n, rows, :]], axis=0)
                hi, lo = pieces(window)
                r1 = dot(ax_ref[...], hi)
                r = r1[0:64] + r1[64:128] + dot(ax_ref[0:64, :], lo)
                out[rows, :] = r[0:32]
                vbuf[rows, :] = r[32:64]

    pp, p4 = lax.rem(me, 4), lax.div(me, 4) * 4

    def turn(f, buf):
        for g in range(2):
            for h in range(2):
                turned[...] = buf[g * 128 : g * 128 + 128, h * 128 : h * 128 + 128].T
                x = [turned[pl.ds(i, 32, stride=4), :] for i in range(4)]
                for t, m in enumerate(lane_blocks(x)):
                    at = ((4 * g + t) * 16 + h * 8) * 4
                    xsend[f, at : at + 32, :] = m
        mine = pltpu.make_async_copy(
            xsend.at[f, pl.ds(me * 4, 4)], xrecv.at[f, pp, pl.ds(p4, 4)], lsem.at[1 + f]
        )
        mine.start()
        return mine

    def turn_copy(f, q):
        return pltpu.make_async_remote_copy(
            src_ref=xsend.at[f, pl.ds(q * 4, 4)],
            dst_ref=xrecv.at[f, pp, pl.ds(p4, 4)],
            send_sem=xsem.at[0, f],
            recv_sem=xsem.at[1, f],
            device_id=(q, lev),
            device_id_type=MESH,
        )

    def turn_wait(f, mine):
        mine.wait()
        every = xsend.at[f, pl.ds(0, 4 * (PENCILS - 1))]
        whole = pltpu.make_async_remote_copy(
            src_ref=every,
            dst_ref=every,
            send_sem=xsem.at[0, f],
            recv_sem=xsem.at[1, f],
            device_id=(right, lev),
            device_id_type=MESH,
        )
        whole.wait_send()
        whole.wait_recv()

    hops0 = halo(0, wd)
    along_x(0, hops0, bbuf)
    bb_f[...] = std[...] * dot(y_operand(vbuf[...]), ty[...])
    own_b = turn(0, bbuf)
    y0 = observe(bb_f[...], lambda q: turn_copy(0, q).start())
    hops1 = halo(1, wgt * y0)
    along_x(1, hops1, ubuf)
    own_u = turn(1, ubuf)
    bu_f[...] = std[...] * dot(y_operand(vbuf[...]), ty[...])
    y1 = observe(bu_f[...], lambda q: turn_copy(1, q).start())

    def fold(v):
        return jnp.sum(v.reshape(32, 8, 256), axis=0)

    def cells_row(p):
        p = fold(p)
        return jnp.sum(p[:, 0:128] + p[:, 128:256], axis=0, keepdims=True)

    def obs_row(p):
        return p[:, 0:128] + p[:, 128:256] + p[:, 256:384] + p[:, 384:512]

    b, u = bbuf[...], ubuf[...]
    rows6 = [
        cells_row(b * b), cells_row(b * u), cells_row(u * u),
        obs_row(wgt * y0 * y0), obs_row(wgt * y0 * y1), obs_row(wgt * y1 * y1),
    ]
    sub = lax.broadcasted_iota(I32, (8, 128), 0)
    stack = jnp.zeros((8, 128), F32)
    for i, r in enumerate(rows6):
        stack = jnp.where(sub == i, r, stack)
    sums = jnp.sum(stack, axis=1, keepdims=True)
    diagonal = sub == lax.broadcasted_iota(I32, (8, 128), 1)
    local = jnp.sum(jnp.where(diagonal, sums, 0.0), axis=0, keepdims=True)

    def sum_over(mine, n, count, send, recv, sem, targets):
        send[0] = mine
        recv[n] = mine

        def copy(to, many=False):
            return pltpu.make_async_remote_copy(
                src_ref=recv.at[pl.ds(0, count - 1)] if many else send.at[pl.ds(0, 1)],
                dst_ref=recv.at[pl.ds(0, count - 1)] if many else recv.at[pl.ds(n, 1)],
                send_sem=sem.at[0],
                recv_sem=sem.at[1],
                device_id=to,
                device_id_type=MESH,
            )

        for to in targets:
            copy(to).start()
        done = copy(targets[0], True)
        done.wait_send()
        done.wait_recv()
        parts = [recv[i] for i in range(count)]
        while len(parts) > 1:
            parts = [parts[i] + parts[i + 1] for i in range(0, len(parts), 2)]
        return parts[0]

    total = sum_over(local, near, NEAR, asend, arecv, asem, [(row * NEAR + zc, lev) for zc in zcs[:-1]])
    total = sum_over(
        total, row * LEVS + lev, FAR_Y * LEVS, csend, crecv, csem,
        [
            (lax.rem(row + dy, FAR_Y) * NEAR + near, lax.rem(lev + dx, LEVS))
            for dy in (4, 3, 5, 2, 6, 1, 7, 0)
            for dx in (2, 1, 3, 0)
            if dx or dy
        ],
    )
    bb, bu, uu, q00, q01, q11 = [total[:, i : i + 1] for i in range(6)]

    ratio = bu / bb
    alpha0 = 1.0 / (1.0 + ratio)
    norm1 = alpha0 * alpha0 * (uu - ratio * bu)
    gb = ratio * alpha0 + norm1 / bb
    gu = -alpha0
    curve = gb * gb * (bb + q00) + 2.0 * gb * gu * (bu + q01) + gu * gu * (uu + q11)
    alpha1 = norm1 / curve
    c_b = alpha0 + alpha1 * gb
    c_u = alpha1 * gu

    for t in range(8):
        rows = slice(t * 32, t * 32 + 32)
        incr_out[0, :, t * 256 : t * 256 + 256] = c_b * bb_f[rows, :] + c_u * bu_f[rows, :]

    for copies in hops0 + hops1:
        for copy in copies:
            copy.wait_send()
    turn_wait(0, own_b)
    turn_wait(1, own_u)
    got_b = lane_blocks([xrecv[0, i] for i in range(4)])
    got_u = lane_blocks([xrecv[1, i] for i in range(4)])
    for i in range(4):
        ctl[pl.ds(i, 128, stride=4), :] = c_b * got_b[i] + c_u * got_u[i]
    for p in range(32):
        control_out[0, :, p * 128 : p * 128 + 128] = ctl[p * 16 : p * 16 + 16, :]


def body(background_std, x_kernel, y_kernel, obs_owner, obs_cells, obs_weights, innovation, obs_precision, obs_counts):
    holding = obs_owner.shape[0]
    vmem = pl.BlockSpec(memory_space=pltpu.VMEM)
    hbm = pl.BlockSpec(memory_space=pltpu.HBM)
    field = pltpu.VMEM((256, 256), F32)
    dma = pltpu.SemaphoreType.DMA
    keep = lambda x: pltpu.with_memory_space_constraint(x, pltpu.HBM)
    return pl.pallas_call(
        kernel,
        out_shape=(
            jax.ShapeDtypeStruct((1, 16, 4096), F32),
            jax.ShapeDtypeStruct((1, 32, 2048), F32),
        ),
        in_specs=[hbm] * 9,
        out_specs=(vmem, vmem),
        scratch_shapes=[
            pltpu.VMEM((1, 32, 2048), F32), pltpu.SMEM((1, 31), F32), pltpu.SMEM((1, 31), F32),
            pltpu.VMEM((1, holding), I32), pltpu.VMEM((16, holding), I32), pltpu.VMEM((16, holding), F32),
            pltpu.VMEM((1, holding), F32), pltpu.VMEM((1, holding), F32), pltpu.SMEM((1, 1), I32),
            pltpu.VMEM((256, 128), F32), pltpu.VMEM((256, 128), F32),
            pltpu.VMEM((256, 128), F32),
            pltpu.VMEM((16, 512), F32), pltpu.VMEM((16, 512), F32), pltpu.VMEM((16, 512), F32),
            pltpu.VMEM((4, 256, 2048), BF16),
            pltpu.VMEM((1152, 256), BF16), pltpu.VMEM((1152, 256), BF16),
            pltpu.VMEM((128, 96), BF16),
            field,
            pltpu.VMEM((512, 256), BF16),
            pltpu.VMEM((512, 256), F32),
            pltpu.VMEM((2, 256, 256), F32), pltpu.VMEM((2, 256, 256), F32), pltpu.VMEM((2, 256, 256), F32),
            field, field, field, field, field,
            pltpu.VMEM((128, 128), F32), pltpu.VMEM((512, 128), F32),
            pltpu.VMEM((2, 512, 128), F32), pltpu.VMEM((2, 4, 128, 128), F32),
            pltpu.VMEM((1, 1, 128), F32), pltpu.VMEM((NEAR, 1, 128), F32),
            pltpu.VMEM((1, 1, 128), F32), pltpu.VMEM((FAR_Y * LEVS, 1, 128), F32),
            dma((9,)), dma((2,)), dma((2, 2, CHUNKS)), dma((2, 2, CHUNKS)), dma((2, 2)), dma((2,)), dma((2,)), dma((3,)),
        ],
        compiler_params=pltpu.CompilerParams(
            collective_id=0, has_side_effects=True, vmem_limit_bytes=52 << 20
        ),
        name="assimilate",
    )(
        *map(keep, (background_std, x_kernel, y_kernel, obs_owner.reshape(1, holding), obs_cells.T, obs_weights.T,
        innovation.reshape(1, holding), obs_precision.reshape(1, holding))), obs_counts.reshape(1, 1),
    )


def solution(mesh):
    return jax.shard_map(
        body,
        mesh=mesh,
        in_specs=(
            P("lev", "pencil", None),
            P("lev", None),
            P("lev", None),
            P(("pencil", "lev"), None),
            P(("pencil", "lev"), None),
            P(("pencil", "lev"), None),
            P(("pencil", "lev")),
            P(("pencil", "lev")),
            P(("pencil", "lev")),
        ),
        out_specs=(P("lev", "pencil", None), P("lev", "pencil", None)),
        check_vma=False,
    )
```

```python
import functools

import jax
import jax.numpy as jnp
from jax import lax
from jax.experimental import pallas as pl
from jax.experimental.pallas import tpu as pltpu
from jax.sharding import PartitionSpec as P

F32, BF16, I32 = jnp.float32, jnp.bfloat16, jnp.int32
MESH = pl.DeviceIdType.MESH
HALF = 15
PENCILS = 128
LEVS = 4
NEAR = 16
FAR_Y = 8
SLOTS = 4
NT = (((1,), (1,)), ((), ()))
FARTHEST = (8, 7, 9, 6, 10, 5, 11, 4, 12, 3, 13, 2, 14, 1, 15, 0)
CHUNKS = 2
PART = 256 // CHUNKS


def dot(a, b):
    return jnp.dot(a, b, preferred_element_type=F32)


def pieces(v):
    hi = v.astype(BF16)
    return hi, (v - hi.astype(F32)).astype(BF16)


def band(delta, taps, sign):
    out = jnp.zeros(delta.shape, F32)
    for d in range(-HALF, HALF + 1):
        out = jnp.where(delta == d, taps[0, HALF + sign * d], out)
    return out


def lane_blocks(x):
    lane = lax.broadcasted_iota(I32, x[0].shape, x[0].ndim - 1)
    ax = x[0].ndim - 1
    low, even = lane < 64, (lane & 32) == 0

    def halves(a, b):
        return jnp.where(low, a, pltpu.roll(b, 64, ax)), jnp.where(low, pltpu.roll(a, 64, ax), b)

    def quarters(a, b):
        return jnp.where(even, a, pltpu.roll(b, 32, ax)), jnp.where(even, pltpu.roll(a, 96, ax), b)

    a, c = halves(x[0], x[2])
    b, d = halves(x[1], x[3])
    return quarters(a, b) + quarters(c, d)


def kernel(
    std_hbm, xk_hbm, yk_hbm, owner_hbm, cells_hbm, weights_hbm, innov_hbm, prec_hbm, counts_hbm,
    control_out, incr_out,
    std_in, xk, yk, owner, cells, weights, innov, prec, counts,
    osend, orecv, rt_ref, hi_ref, lo_ref, w_ref, lot,
    ty, tyt, ax_ref, std, g2, acc,
    fown, fl, fr, vbuf, bbuf, ubuf, bb_f, bu_f,
    turned, ctl, xsend, xrecv, asend, arecv, csend, crecv,
    isem, osem, hsem_s, hsem_r, xsem, asem, csem, lsem,
):
    me = lax.axis_index("pencil")
    lev = lax.axis_index("lev")
    near = lax.rem(me, NEAR)
    row = lax.div(me, NEAR)
    left, right = lax.rem(me + PENCILS - 1, PENCILS), lax.rem(me + 1, PENCILS)
    zcs = [lax.rem(near + j, NEAR) for j in FARTHEST]

    def peer_row(i):
        dy = FAR_Y // 2 + lax.div(i + 1, 2) * (1 - 2 * lax.rem(i, 2))
        return lax.rem(row + dy, FAR_Y) * NEAR

    def each_peer(act):
        @pl.loop(0, FAR_Y - 1)
        def _(i):
            base = peer_row(i)
            for zc in zcs:
                act(base + zc)

        for zc in zcs[:-1]:
            act(row * NEAR + zc)

    loads = [
        pltpu.make_async_copy(src, dst, isem.at[i])
        for i, (src, dst) in enumerate(
            (
                (owner_hbm, owner), (prec_hbm, prec), (innov_hbm, innov), (counts_hbm, counts),
                (cells_hbm, cells), (weights_hbm, weights), (xk_hbm, xk), (yk_hbm, yk), (std_hbm, std_in),
            )
        )
    ]
    for load in loads:
        load.start()
    barrier = pltpu.get_barrier_semaphore()

    def hello(q, to_lev=lev):
        pl.semaphore_signal(barrier, inc=1, device_id=(q, to_lev), device_id_type=MESH)

    each_peer(hello)

    @pl.loop(0, FAR_Y)
    def _(i):
        for dx in (2, 1, 3):
            hello(lax.rem(row + FAR_Y // 2 + i, FAR_Y) * NEAR + near, lax.rem(lev + dx, LEVS))

    for load in loads[:6]:
        load.wait()

    n_obs = cells.shape[1]
    lane_o = lax.broadcasted_iota(I32, (1, n_obs), 1)
    weight = jnp.where(lane_o < counts[0, 0], prec[...], 0.0)
    member = lax.broadcasted_iota(I32, (PENCILS, n_obs), 0) == owner[...]
    member_b = jnp.where(member, 1.0, 0.0).astype(BF16)
    before = lax.broadcasted_iota(I32, (n_obs, n_obs), 0) < lax.broadcasted_iota(I32, (n_obs, n_obs), 1)
    rank = dot(member_b, jnp.where(before, 1.0, 0.0).astype(BF16))
    sub8 = lax.broadcasted_iota(I32, (8, n_obs), 0)
    tail = jnp.where(sub8 == 0, weight * innov[...], jnp.where(sub8 == 1, weight, 0.0))
    feats = jnp.concatenate(
        [cells[...].astype(F32), weights[...], tail, jnp.zeros((24, n_obs), F32)], axis=0
    )
    f0 = feats.astype(BF16)
    rest = feats - f0.astype(F32)
    f1 = rest.astype(BF16)
    f2 = (rest - f1.astype(F32)).astype(BF16)
    packed = []
    for s in range(SLOTS):
        pick = jnp.where(member, jnp.where(rank == float(s), 1.0, 0.0), 0.0).astype(BF16)
        parts = [lax.dot_general(pick, f, NT, preferred_element_type=F32) for f in (f0, f1, f2)]
        packed.append(parts[0] + parts[1] + parts[2])
    for h in range(2):
        osend[pl.ds(h, PENCILS, stride=2), :] = jnp.concatenate(packed[2 * h : 2 * h + 2], axis=1)

    pl.semaphore_wait(barrier, PENCILS - 1 + FAR_Y * (LEVS - 1))

    own = pltpu.make_async_copy(osend.at[pl.ds(me * 2, 2)], orecv.at[pl.ds(me * 2, 2)], lsem.at[0])
    own.start()

    def obs_copy(q, n=1):
        return pltpu.make_async_remote_copy(
            src_ref=osend.at[pl.ds(q * 2, 2 * n)],
            dst_ref=orecv.at[pl.ds((me if n == 1 else 0) * 2, 2 * n)],
            send_sem=osem.at[0],
            recv_sem=osem.at[1],
            device_id=(q if n == 1 else right, lev),
            device_id_type=MESH,
        )

    each_peer(lambda q: obs_copy(q).start())
    for load in loads[6:]:
        load.wait()

    base_delta = lax.broadcasted_iota(I32, (8, 512), 0) - lax.broadcasted_iota(I32, (8, 512), 1) + 256
    for sign, ref in ((1, ty), (-1, tyt)):
        base = band(base_delta, yk, sign)
        for g in range(48):
            p0 = 8 * g if g < 40 else 8 * g - 384
            r = pltpu.roll(base, (p0 - 256) % 512, 1)[:, :256]
            acc[8 * g : 8 * g + 8, :] = r
        hi, lo = pieces(acc[0:384, :])
        ref[0:384, :] = hi
        ref[384:768, :] = hi
        ref[768:1152, :] = lo
    delta = lax.broadcasted_iota(I32, (32, 96), 1) - lax.broadcasted_iota(I32, (32, 96), 0) - 32
    delta_w = lax.broadcasted_iota(I32, (96, 96), 1) - lax.broadcasted_iota(I32, (96, 96), 0)
    a1 = band(delta, xk, -1)
    a2 = jnp.dot(
        band(delta, xk, 1),
        band(delta_w, xk, -1),
        preferred_element_type=F32,
        precision=lax.Precision.HIGHEST,
    )
    a_hi, a_lo = pieces(jnp.concatenate([a1, a2], axis=0))
    ax_ref[0:64, :] = a_hi
    ax_ref[64:128, :] = a_lo
    for t in range(8):
        std[t * 32 : t * 32 + 32, :] = std_in[0, :, t * 256 : t * 256 + 256]

    own.wait()
    everyone = obs_copy(0, PENCILS - 1)
    everyone.wait_send()
    everyone.wait_recv()

    for h in range(2):
        rt_ref[h * 128 : h * 128 + 128, :] = orecv[pl.ds(h, PENCILS, stride=2), :].T
    wd, wgt = [], []
    for s in range(SLOTS):
        c = rt_ref[s * 64 : s * 64 + 16, :].astype(I32)
        cols = slice(s * 128, s * 128 + 128)
        hi_ref[:, cols] = (((c >> 8) & 7) * 32 + (c >> 11)).astype(F32)
        lo_ref[:, cols] = (c & 255).astype(F32)
        w_ref[:, cols] = rt_ref[s * 64 + 16 : s * 64 + 32, :]
        wd.append(rt_ref[s * 64 + 32 : s * 64 + 33, :])
        wgt.append(rt_ref[s * 64 + 33 : s * 64 + 34, :])
    wd, wgt = jnp.concatenate(wd, axis=1), jnp.concatenate(wgt, axis=1)
    iota_f = lax.broadcasted_iota(I32, (256, 128), 0).astype(F32)
    iota_b = iota_f.astype(BF16)
    iota_b4 = jnp.concatenate([iota_b] * 4, axis=1)
    iota_f4 = jnp.concatenate([iota_f] * 4, axis=1)
    one, zero = jnp.bfloat16(1), jnp.bfloat16(0)

    def spread(z, first):
        acc[...] = jnp.zeros_like(acc)

        @pl.loop(0, 4)
        def _(n):
            lhs = []
            for j in range(4):
                k = n * 4 + j
                if first:
                    lo = lo_ref[pl.ds(k, 1), :].astype(BF16)
                    lot[n, :, j * 512 : j * 512 + 512] = jnp.where(iota_b4 == lo, one, zero)
                hit = iota_b4 == hi_ref[pl.ds(k, 1), :].astype(BF16)
                z_hi, z_lo = pieces(w_ref[pl.ds(k, 1), :] * z)
                lhs.append(jnp.concatenate([jnp.where(hit, z_hi, zero), jnp.where(hit, z_lo, zero)], axis=0))
            acc[...] += lax.dot_general(jnp.concatenate(lhs, axis=1), lot[n], NT, preferred_element_type=F32)

        return acc[0:256, :] + acc[256:512, :]

    def observe(field):
        g_hi, g_lo = pieces(field)
        g2[0:256, :] = g_hi
        g2[256:512, :] = g_lo
        def step(n, total):
            both = dot(g2[...], lot[n])
            for j in range(4):
                k = n * 4 + j
                t = both[:, j * 512 : j * 512 + 512]
                found = jnp.where(iota_f4 == hi_ref[pl.ds(k, 1), :], t[0:256] + t[256:512], 0.0)
                total += w_ref[pl.ds(k, 1), :] * jnp.sum(found.reshape(32, 8, 512), axis=0)
            return total

        total = lax.fori_loop(0, 4, step, jnp.zeros((8, 512), F32))
        return jnp.sum(total, axis=0, keepdims=True)

    edge_low = lax.broadcasted_iota(I32, (256, 128), 1) < 64

    def y_operand(g):
        blank = jnp.zeros((32, 128), F32)
        up = jnp.concatenate([g[32:, 0:128], blank], axis=0)
        down = jnp.concatenate([blank, g[:224, 128:256]], axis=0)
        hi, lo = pieces(jnp.concatenate([g, jnp.where(edge_low, up, down)], axis=1))
        return jnp.concatenate([hi, lo, hi], axis=1)

    def halo(n, z):
        operand = y_operand(std[...] * spread(z, n == 0))
        copies = []
        for c in range(CHUNKS):
            rows = slice(c * PART, c * PART + PART)
            fown[n, rows, :] = dot(operand[rows], tyt[...])
            both = []
            for side, (to, dst) in enumerate(((left, fr), (right, fl))):
                both.append(
                    pltpu.make_async_remote_copy(
                        src_ref=fown.at[n, pl.ds(c * PART, PART)],
                        dst_ref=dst.at[n, pl.ds(c * PART, PART)],
                        send_sem=hsem_s.at[n, side, c],
                        recv_sem=hsem_r.at[n, side, c],
                        device_id=(to, lev),
                        device_id_type=MESH,
                    )
                )
                both[-1].start()
            copies.append(both)
        return copies

    def along_x(n, copies, out):
        for c in range(CHUNKS):
            for copy in copies[c]:
                copy.wait_recv()
            for t in range(c * 8 // CHUNKS, (c + 1) * 8 // CHUNKS):
                rows = slice(t * 32, t * 32 + 32)
                window = jnp.concatenate([fl[n, rows, :], fown[n, rows, :], fr[n, rows, :]], axis=0)
                hi, lo = pieces(window)
                r1 = dot(ax_ref[...], hi)
                r = r1[0:64] + r1[64:128] + dot(ax_ref[0:64, :], lo)
                out[rows, :] = r[0:32]
                vbuf[rows, :] = r[32:64]

    pp, p4 = lax.rem(me, 4), lax.div(me, 4) * 4

    def turn(f, buf):
        for g in range(2):
            for h in range(2):
                turned[...] = buf[g * 128 : g * 128 + 128, h * 128 : h * 128 + 128].T
                x = [turned[pl.ds(i, 32, stride=4), :] for i in range(4)]
                for t, m in enumerate(lane_blocks(x)):
                    at = ((4 * g + t) * 16 + h * 8) * 4
                    xsend[f, at : at + 32, :] = m
        mine = pltpu.make_async_copy(
            xsend.at[f, pl.ds(me * 4, 4)], xrecv.at[f, pp, pl.ds(p4, 4)], lsem.at[1 + f]
        )
        mine.start()
        each_peer(lambda q: turn_copy(f, q).start())
        return mine

    def turn_copy(f, q):
        return pltpu.make_async_remote_copy(
            src_ref=xsend.at[f, pl.ds(q * 4, 4)],
            dst_ref=xrecv.at[f, pp, pl.ds(p4, 4)],
            send_sem=xsem.at[0, f],
            recv_sem=xsem.at[1, f],
            device_id=(q, lev),
            device_id_type=MESH,
        )

    def turn_wait(f, mine):
        mine.wait()
        every = xsend.at[f, pl.ds(0, 4 * (PENCILS - 1))]
        whole = pltpu.make_async_remote_copy(
            src_ref=every,
            dst_ref=every,
            send_sem=xsem.at[0, f],
            recv_sem=xsem.at[1, f],
            device_id=(right, lev),
            device_id_type=MESH,
        )
        whole.wait_send()
        whole.wait_recv()
        for i, m in enumerate(lane_blocks([xrecv[f, i] for i in range(4)])):
            ctl[f, pl.ds(i, 128, stride=4), :] = m

    hops0 = halo(0, wd)
    along_x(0, hops0, bbuf)
    bb_f[...] = std[...] * dot(y_operand(vbuf[...]), ty[...])
    own_b = turn(0, bbuf)
    y0 = observe(bb_f[...])
    hops1 = halo(1, wgt * y0)
    along_x(1, hops1, ubuf)
    bu_f[...] = std[...] * dot(y_operand(vbuf[...]), ty[...])
    y1 = observe(bu_f[...])

    def fold(v):
        return jnp.sum(v.reshape(32, 8, 256), axis=0)

    def cells_row(p):
        p = fold(p)
        return jnp.sum(p[:, 0:128] + p[:, 128:256], axis=0, keepdims=True)

    def obs_row(p):
        return p[:, 0:128] + p[:, 128:256] + p[:, 256:384] + p[:, 384:512]

    b, u = bbuf[...], ubuf[...]
    rows6 = [
        cells_row(b * b), cells_row(b * u), cells_row(u * u),
        obs_row(wgt * y0 * y0), obs_row(wgt * y0 * y1), obs_row(wgt * y1 * y1),
    ]
    sub = lax.broadcasted_iota(I32, (8, 128), 0)
    stack = jnp.zeros((8, 128), F32)
    for i, r in enumerate(rows6):
        stack = jnp.where(sub == i, r, stack)
    sums = jnp.sum(stack, axis=1, keepdims=True)
    diagonal = sub == lax.broadcasted_iota(I32, (8, 128), 1)
    local = jnp.sum(jnp.where(diagonal, sums, 0.0), axis=0, keepdims=True)

    def sum_over(mine, n, count, send, recv, sem, targets, meanwhile=None):
        send[0] = mine
        recv[n] = mine

        def copy(to, many=False):
            return pltpu.make_async_remote_copy(
                src_ref=recv.at[pl.ds(0, count - 1)] if many else send.at[pl.ds(0, 1)],
                dst_ref=recv.at[pl.ds(0, count - 1)] if many else recv.at[pl.ds(n, 1)],
                send_sem=sem.at[0],
                recv_sem=sem.at[1],
                device_id=to,
                device_id_type=MESH,
            )

        for to in targets:
            copy(to).start()
        if meanwhile:
            meanwhile()
        done = copy(targets[0], True)
        done.wait_send()
        done.wait_recv()
        parts = [recv[i] for i in range(count)]
        while len(parts) > 1:
            parts = [parts[i] + parts[i + 1] for i in range(0, len(parts), 2)]
        return parts[0]

    own_u = []
    total = sum_over(
        local, near, NEAR, asend, arecv, asem, [(row * NEAR + zc, lev) for zc in zcs[:-1]],
        lambda: own_u.append(turn(1, ubuf)),
    )
    total = sum_over(
        total, row * LEVS + lev, FAR_Y * LEVS, csend, crecv, csem,
        [
            (lax.rem(row + dy, FAR_Y) * NEAR + near, lax.rem(lev + dx, LEVS))
            for dy in (4, 3, 5, 2, 6, 1, 7, 0)
            for dx in (2, 1, 3, 0)
            if dx or dy
        ],
        lambda: turn_wait(0, own_b),
    )
    bb, bu, uu, q00, q01, q11 = [total[:, i : i + 1] for i in range(6)]

    ratio = bu / bb
    alpha0 = 1.0 / (1.0 + ratio)
    norm1 = alpha0 * alpha0 * (uu - ratio * bu)
    gb = ratio * alpha0 + norm1 / bb
    gu = -alpha0
    curve = gb * gb * (bb + q00) + 2.0 * gb * gu * (bu + q01) + gu * gu * (uu + q11)
    alpha1 = norm1 / curve
    c_b = alpha0 + alpha1 * gb
    c_u = alpha1 * gu

    for t in range(8):
        rows = slice(t * 32, t * 32 + 32)
        incr_out[0, :, t * 256 : t * 256 + 256] = c_b * bb_f[rows, :] + c_u * bu_f[rows, :]

    for copies in hops0 + hops1:
        for copy in copies:
            copy.wait_send()
    turn_wait(1, own_u[0])
    for p in range(32):
        rows = slice(p * 16, p * 16 + 16)
        control_out[0, :, p * 128 : p * 128 + 128] = c_b * ctl[0, rows, :] + c_u * ctl[1, rows, :]


def body(background_std, x_kernel, y_kernel, obs_owner, obs_cells, obs_weights, innovation, obs_precision, obs_counts):
    holding = obs_owner.shape[0]
    vmem = pl.BlockSpec(memory_space=pltpu.VMEM)
    hbm = pl.BlockSpec(memory_space=pltpu.HBM)
    field = pltpu.VMEM((256, 256), F32)
    dma = pltpu.SemaphoreType.DMA
    keep = lambda x: pltpu.with_memory_space_constraint(x, pltpu.HBM)
    return pl.pallas_call(
        kernel,
        out_shape=(
            jax.ShapeDtypeStruct((1, 16, 4096), F32),
            jax.ShapeDtypeStruct((1, 32, 2048), F32),
        ),
        in_specs=[hbm] * 9,
        out_specs=(vmem, vmem),
        scratch_shapes=[
            pltpu.VMEM((1, 32, 2048), F32), pltpu.SMEM((1, 31), F32), pltpu.SMEM((1, 31), F32),
            pltpu.VMEM((1, holding), I32), pltpu.VMEM((16, holding), I32), pltpu.VMEM((16, holding), F32),
            pltpu.VMEM((1, holding), F32), pltpu.VMEM((1, holding), F32), pltpu.SMEM((1, 1), I32),
            pltpu.VMEM((256, 128), F32), pltpu.VMEM((256, 128), F32),
            pltpu.VMEM((256, 128), F32),
            pltpu.VMEM((16, 512), F32), pltpu.VMEM((16, 512), F32), pltpu.VMEM((16, 512), F32),
            pltpu.VMEM((4, 256, 2048), BF16),
            pltpu.VMEM((1152, 256), BF16), pltpu.VMEM((1152, 256), BF16),
            pltpu.VMEM((128, 96), BF16),
            field,
            pltpu.VMEM((512, 256), BF16),
            pltpu.VMEM((512, 256), F32),
            pltpu.VMEM((2, 256, 256), F32), pltpu.VMEM((2, 256, 256), F32), pltpu.VMEM((2, 256, 256), F32),
            field, field, field, field, field,
            pltpu.VMEM((128, 128), F32), pltpu.VMEM((2, 512, 128), F32),
            pltpu.VMEM((2, 512, 128), F32), pltpu.VMEM((2, 4, 128, 128), F32),
            pltpu.VMEM((1, 1, 128), F32), pltpu.VMEM((NEAR, 1, 128), F32),
            pltpu.VMEM((1, 1, 128), F32), pltpu.VMEM((FAR_Y * LEVS, 1, 128), F32),
            dma((9,)), dma((2,)), dma((2, 2, CHUNKS)), dma((2, 2, CHUNKS)), dma((2, 2)), dma((2,)), dma((2,)), dma((3,)),
        ],
        compiler_params=pltpu.CompilerParams(
            collective_id=0, has_side_effects=True, vmem_limit_bytes=52 << 20
        ),
        name="assimilate",
    )(
        *map(keep, (background_std, x_kernel, y_kernel, obs_owner.reshape(1, holding), obs_cells.T, obs_weights.T,
        innovation.reshape(1, holding), obs_precision.reshape(1, holding))), obs_counts.reshape(1, 1),
    )


def solution(mesh):
    return jax.shard_map(
        body,
        mesh=mesh,
        in_specs=(
            P("lev", "pencil", None),
            P("lev", None),
            P("lev", None),
            P(("pencil", "lev"), None),
            P(("pencil", "lev"), None),
            P(("pencil", "lev"), None),
            P(("pencil", "lev")),
            P(("pencil", "lev")),
            P(("pencil", "lev")),
        ),
        out_specs=(P("lev", "pencil", None), P("lev", "pencil", None)),
        check_vma=False,
    )
```

```python
import functools

import jax
import jax.numpy as jnp
from jax import lax
from jax.experimental import pallas as pl
from jax.experimental.pallas import tpu as pltpu
from jax.sharding import PartitionSpec as P

F32, BF16, I32 = jnp.float32, jnp.bfloat16, jnp.int32
MESH = pl.DeviceIdType.MESH
HALF = 15
PENCILS = 128
LEVS = 4
NEAR = 16
FAR_Y = 8
SLOTS = 4
NT = (((1,), (1,)), ((), ()))
FARTHEST = (8, 7, 9, 6, 10, 5, 11, 4, 12, 3, 13, 2, 14, 1, 15, 0)
CHUNKS = 2
PART = 256 // CHUNKS


def dot(a, b):
    return jnp.dot(a, b, preferred_element_type=F32)


def pieces(v):
    hi = v.astype(BF16)
    return hi, (v - hi.astype(F32)).astype(BF16)


def band(delta, taps, sign):
    out = jnp.zeros(delta.shape, F32)
    for d in range(-HALF, HALF + 1):
        out = jnp.where(delta == d, taps[0, HALF + sign * d], out)
    return out


def lane_blocks(x):
    lane = lax.broadcasted_iota(I32, x[0].shape, x[0].ndim - 1)
    ax = x[0].ndim - 1
    low, even = lane < 64, (lane & 32) == 0

    def halves(a, b):
        return jnp.where(low, a, pltpu.roll(b, 64, ax)), jnp.where(low, pltpu.roll(a, 64, ax), b)

    def quarters(a, b):
        return jnp.where(even, a, pltpu.roll(b, 32, ax)), jnp.where(even, pltpu.roll(a, 96, ax), b)

    a, c = halves(x[0], x[2])
    b, d = halves(x[1], x[3])
    return quarters(a, b) + quarters(c, d)


def kernel(
    std_hbm, xk_hbm, yk_hbm, owner_hbm, cells_hbm, weights_hbm, innov_hbm, prec_hbm, counts_hbm,
    control_out, incr_out,
    std_in, xk, yk, owner, cells, weights, innov, prec, counts,
    osend, orecv, rt_ref, hi_ref, lo_ref, w_ref, lot,
    ty, tyt, ax_ref, std, g2, acc,
    fown, fl, fr, vbuf, bbuf, ubuf, bb_f, bu_f,
    turned, ctl, xsend, xrecv, asend, arecv, csend, crecv,
    isem, osem, hsem_s, hsem_r, xsem, asem, csem, lsem,
):
    me = lax.axis_index("pencil")
    lev = lax.axis_index("lev")
    near = lax.rem(me, NEAR)
    row = lax.div(me, NEAR)
    left, right = lax.rem(me + PENCILS - 1, PENCILS), lax.rem(me + 1, PENCILS)
    zcs = [lax.rem(near + j, NEAR) for j in FARTHEST]

    def peer_row(i):
        dy = FAR_Y // 2 + lax.div(i + 1, 2) * (1 - 2 * lax.rem(i, 2))
        return lax.rem(row + dy, FAR_Y) * NEAR

    def each_peer(act):
        @pl.loop(0, FAR_Y - 1)
        def _(i):
            base = peer_row(i)
            for zc in zcs:
                act(base + zc)

        for zc in zcs[:-1]:
            act(row * NEAR + zc)

    barrier = pltpu.get_barrier_semaphore()

    def hello(q, to_lev=lev):
        pl.semaphore_signal(barrier, inc=1, device_id=(q, to_lev), device_id_type=MESH)

    each_peer(hello)

    @pl.loop(0, FAR_Y)
    def _(i):
        for dx in (2, 1, 3):
            hello(lax.rem(row + FAR_Y // 2 + i, FAR_Y) * NEAR + near, lax.rem(lev + dx, LEVS))

    loads = [
        pltpu.make_async_copy(src, dst, isem.at[i])
        for i, (src, dst) in enumerate(
            (
                (owner_hbm, owner), (prec_hbm, prec), (innov_hbm, innov), (counts_hbm, counts),
                (cells_hbm, cells), (weights_hbm, weights), (xk_hbm, xk), (yk_hbm, yk), (std_hbm, std_in),
            )
        )
    ]
    for load in loads:
        load.start()
    for load in loads[:6]:
        load.wait()

    n_obs = cells.shape[1]
    lane_o = lax.broadcasted_iota(I32, (1, n_obs), 1)
    weight = jnp.where(lane_o < counts[0, 0], prec[...], 0.0)
    member = lax.broadcasted_iota(I32, (PENCILS, n_obs), 0) == owner[...]
    member_b = jnp.where(member, 1.0, 0.0).astype(BF16)
    before = lax.broadcasted_iota(I32, (n_obs, n_obs), 0) < lax.broadcasted_iota(I32, (n_obs, n_obs), 1)
    rank = dot(member_b, jnp.where(before, 1.0, 0.0).astype(BF16))
    sub8 = lax.broadcasted_iota(I32, (8, n_obs), 0)
    tail = jnp.where(sub8 == 0, weight * innov[...], jnp.where(sub8 == 1, weight, 0.0))
    feats = jnp.concatenate(
        [cells[...].astype(F32), weights[...], tail, jnp.zeros((24, n_obs), F32)], axis=0
    )
    f0 = feats.astype(BF16)
    rest = feats - f0.astype(F32)
    f1 = rest.astype(BF16)
    f2 = (rest - f1.astype(F32)).astype(BF16)
    packed = []
    for s in range(SLOTS):
        pick = jnp.where(member, jnp.where(rank == float(s), 1.0, 0.0), 0.0).astype(BF16)
        parts = [lax.dot_general(pick, f, NT, preferred_element_type=F32) for f in (f0, f1, f2)]
        packed.append(parts[0] + parts[1] + parts[2])
    for h in range(2):
        osend[pl.ds(h, PENCILS, stride=2), :] = jnp.concatenate(packed[2 * h : 2 * h + 2], axis=1)

    pl.semaphore_wait(barrier, PENCILS - 1 + FAR_Y * (LEVS - 1))

    own = pltpu.make_async_copy(osend.at[pl.ds(me * 2, 2)], orecv.at[pl.ds(me * 2, 2)], lsem.at[0])
    own.start()

    def obs_copy(q, n=1):
        return pltpu.make_async_remote_copy(
            src_ref=osend.at[pl.ds(q * 2, 2 * n)],
            dst_ref=orecv.at[pl.ds((me if n == 1 else 0) * 2, 2 * n)],
            send_sem=osem.at[0],
            recv_sem=osem.at[1],
            device_id=(q if n == 1 else right, lev),
            device_id_type=MESH,
        )

    each_peer(lambda q: obs_copy(q).start())
    for load in loads[6:]:
        load.wait()

    base_delta = lax.broadcasted_iota(I32, (8, 512), 0) - lax.broadcasted_iota(I32, (8, 512), 1) + 256
    for sign, ref in ((1, ty), (-1, tyt)):
        base = band(base_delta, yk, sign)
        for g in range(48):
            p0 = 8 * g if g < 40 else 8 * g - 384
            r = pltpu.roll(base, (p0 - 256) % 512, 1)[:, :256]
            acc[8 * g : 8 * g + 8, :] = r
        hi, lo = pieces(acc[0:384, :])
        ref[0:384, :] = hi
        ref[384:768, :] = hi
        ref[768:1152, :] = lo
    delta = lax.broadcasted_iota(I32, (32, 96), 1) - lax.broadcasted_iota(I32, (32, 96), 0) - 32
    delta_w = lax.broadcasted_iota(I32, (96, 96), 1) - lax.broadcasted_iota(I32, (96, 96), 0)
    a1 = band(delta, xk, -1)
    a2 = jnp.dot(
        band(delta, xk, 1),
        band(delta_w, xk, -1),
        preferred_element_type=F32,
        precision=lax.Precision.HIGHEST,
    )
    a_hi, a_lo = pieces(jnp.concatenate([a1, a2], axis=0))
    ax_ref[0:64, :] = a_hi
    ax_ref[64:128, :] = a_lo
    for t in range(8):
        std[t * 32 : t * 32 + 32, :] = std_in[0, :, t * 256 : t * 256 + 256]

    own.wait()
    everyone = obs_copy(0, PENCILS - 1)
    everyone.wait_send()
    everyone.wait_recv()

    for h in range(2):
        rt_ref[h * 128 : h * 128 + 128, :] = orecv[pl.ds(h, PENCILS, stride=2), :].T
    wd, wgt = [], []
    for s in range(SLOTS):
        c = rt_ref[s * 64 : s * 64 + 16, :].astype(I32)
        cols = slice(s * 128, s * 128 + 128)
        hi_ref[:, cols] = (((c >> 8) & 7) * 32 + (c >> 11)).astype(F32)
        lo_ref[:, cols] = (c & 255).astype(F32)
        w_ref[:, cols] = rt_ref[s * 64 + 16 : s * 64 + 32, :]
        wd.append(rt_ref[s * 64 + 32 : s * 64 + 33, :])
        wgt.append(rt_ref[s * 64 + 33 : s * 64 + 34, :])
    wd, wgt = jnp.concatenate(wd, axis=1), jnp.concatenate(wgt, axis=1)
    iota_f = lax.broadcasted_iota(I32, (256, 128), 0).astype(F32)
    iota_b = iota_f.astype(BF16)
    iota_b4 = jnp.concatenate([iota_b] * 4, axis=1)
    iota_f4 = jnp.concatenate([iota_f] * 4, axis=1)
    one, zero = jnp.bfloat16(1), jnp.bfloat16(0)

    def spread(z, first):
        acc[...] = jnp.zeros_like(acc)

        @pl.loop(0, 4)
        def _(n):
            lhs = []
            for j in range(4):
                k = n * 4 + j
                if first:
                    lo = lo_ref[pl.ds(k, 1), :].astype(BF16)
                    lot[n, :, j * 512 : j * 512 + 512] = jnp.where(iota_b4 == lo, one, zero)
                hit = iota_b4 == hi_ref[pl.ds(k, 1), :].astype(BF16)
                z_hi, z_lo = pieces(w_ref[pl.ds(k, 1), :] * z)
                lhs.append(jnp.concatenate([jnp.where(hit, z_hi, zero), jnp.where(hit, z_lo, zero)], axis=0))
            acc[...] += lax.dot_general(jnp.concatenate(lhs, axis=1), lot[n], NT, preferred_element_type=F32)

        return acc[0:256, :] + acc[256:512, :]

    def observe(field):
        g_hi, g_lo = pieces(field)
        g2[0:256, :] = g_hi
        g2[256:512, :] = g_lo
        def step(n, total):
            both = dot(g2[...], lot[n])
            for j in range(4):
                k = n * 4 + j
                t = both[:, j * 512 : j * 512 + 512]
                found = jnp.where(iota_f4 == hi_ref[pl.ds(k, 1), :], t[0:256] + t[256:512], 0.0)
                total += w_ref[pl.ds(k, 1), :] * jnp.sum(found.reshape(32, 8, 512), axis=0)
            return total

        total = lax.fori_loop(0, 4, step, jnp.zeros((8, 512), F32))
        return jnp.sum(total, axis=0, keepdims=True)

    edge_low = lax.broadcasted_iota(I32, (256, 128), 1) < 64

    def y_operand(g):
        blank = jnp.zeros((32, 128), F32)
        up = jnp.concatenate([g[32:, 0:128], blank], axis=0)
        down = jnp.concatenate([blank, g[:224, 128:256]], axis=0)
        hi, lo = pieces(jnp.concatenate([g, jnp.where(edge_low, up, down)], axis=1))
        return jnp.concatenate([hi, lo, hi], axis=1)

    def halo(n, z):
        operand = y_operand(std[...] * spread(z, n == 0))
        copies = []
        for c in range(CHUNKS):
            rows = slice(c * PART, c * PART + PART)
            fown[n, rows, :] = dot(operand[rows], tyt[...])
            both = []
            for side, (to, dst) in enumerate(((left, fr), (right, fl))):
                both.append(
                    pltpu.make_async_remote_copy(
                        src_ref=fown.at[n, pl.ds(c * PART, PART)],
                        dst_ref=dst.at[n, pl.ds(c * PART, PART)],
                        send_sem=hsem_s.at[n, side, c],
                        recv_sem=hsem_r.at[n, side, c],
                        device_id=(to, lev),
                        device_id_type=MESH,
                    )
                )
                both[-1].start()
            copies.append(both)
        return copies

    def along_x(n, copies, out, halfway=None):
        for c in range(CHUNKS):
            for copy in copies[c]:
                copy.wait_recv()
            for t in range(c * 8 // CHUNKS, (c + 1) * 8 // CHUNKS):
                rows = slice(t * 32, t * 32 + 32)
                window = jnp.concatenate([fl[n, rows, :], fown[n, rows, :], fr[n, rows, :]], axis=0)
                hi, lo = pieces(window)
                r1 = dot(ax_ref[...], hi)
                r = r1[0:64] + r1[64:128] + dot(ax_ref[0:64, :], lo)
                out[rows, :] = r[0:32]
                vbuf[rows, :] = r[32:64]
            if halfway and 2 * (c + 1) == CHUNKS:
                halfway()

    pp, p4 = lax.rem(me, 4), lax.div(me, 4) * 4

    def turn_half(f, buf, g):
        for h in range(2):
            turned[...] = buf[g * 128 : g * 128 + 128, h * 128 : h * 128 + 128].T
            x = [turned[pl.ds(i, 32, stride=4), :] for i in range(4)]
            for t, m in enumerate(lane_blocks(x)):
                at = ((4 * g + t) * 16 + h * 8) * 4
                xsend[f, at : at + 32, :] = m

    def turn_own(f):
        mine = pltpu.make_async_copy(
            xsend.at[f, pl.ds(me * 4, 4)], xrecv.at[f, pp, pl.ds(p4, 4)], lsem.at[1 + f]
        )
        mine.start()
        return mine

    def turn(f, buf):
        turn_half(f, buf, 0)
        turn_half(f, buf, 1)
        mine = turn_own(f)
        each_peer(lambda q: turn_copy(f, q).start())
        return mine

    def send_half(f, g):
        half = PENCILS // 2

        @pl.loop(0, 7)
        def _(o):
            for j in range(9):
                turn_copy(f, half * g + lax.rem(me + 1 + 9 * o + j, half)).start()

        @pl.when(lax.div(me, half) != g)
        def _():
            turn_copy(f, half * g + lax.rem(me, half)).start()

    def turn_copy(f, q):
        return pltpu.make_async_remote_copy(
            src_ref=xsend.at[f, pl.ds(q * 4, 4)],
            dst_ref=xrecv.at[f, pp, pl.ds(p4, 4)],
            send_sem=xsem.at[0, f],
            recv_sem=xsem.at[1, f],
            device_id=(q, lev),
            device_id_type=MESH,
        )

    def turn_wait(f, mine):
        mine.wait()
        every = xsend.at[f, pl.ds(0, 4 * (PENCILS - 1))]
        whole = pltpu.make_async_remote_copy(
            src_ref=every,
            dst_ref=every,
            send_sem=xsem.at[0, f],
            recv_sem=xsem.at[1, f],
            device_id=(right, lev),
            device_id_type=MESH,
        )
        whole.wait_send()
        whole.wait_recv()
        for i, m in enumerate(lane_blocks([xrecv[f, i] for i in range(4)])):
            ctl[f, pl.ds(i, 128, stride=4), :] = m

    def turn_b(g):
        turn_half(0, bbuf, g)
        send_half(0, g)

    hops0 = halo(0, wd)
    along_x(0, hops0, bbuf, lambda: turn_b(0))
    bb_f[...] = std[...] * dot(y_operand(vbuf[...]), ty[...])
    turn_b(1)
    own_b = turn_own(0)
    y0 = observe(bb_f[...])
    hops1 = halo(1, wgt * y0)
    along_x(1, hops1, ubuf)
    bu_f[...] = std[...] * dot(y_operand(vbuf[...]), ty[...])
    y1 = observe(bu_f[...])

    def fold(v):
        return jnp.sum(v.reshape(32, 8, 256), axis=0)

    def cells_row(p):
        p = fold(p)
        return jnp.sum(p[:, 0:128] + p[:, 128:256], axis=0, keepdims=True)

    def obs_row(p):
        return p[:, 0:128] + p[:, 128:256] + p[:, 256:384] + p[:, 384:512]

    b, u = bbuf[...], ubuf[...]
    rows6 = [
        cells_row(b * b), cells_row(b * u), cells_row(u * u),
        obs_row(wgt * y0 * y0), obs_row(wgt * y0 * y1), obs_row(wgt * y1 * y1),
    ]
    sub = lax.broadcasted_iota(I32, (8, 128), 0)
    stack = jnp.zeros((8, 128), F32)
    for i, r in enumerate(rows6):
        stack = jnp.where(sub == i, r, stack)
    sums = jnp.sum(stack, axis=1, keepdims=True)
    diagonal = sub == lax.broadcasted_iota(I32, (8, 128), 1)
    local = jnp.sum(jnp.where(diagonal, sums, 0.0), axis=0, keepdims=True)

    def sum_over(mine, n, count, send, recv, sem, targets, meanwhile=None):
        send[0] = mine
        recv[n] = mine

        def copy(to, many=False):
            return pltpu.make_async_remote_copy(
                src_ref=recv.at[pl.ds(0, count - 1)] if many else send.at[pl.ds(0, 1)],
                dst_ref=recv.at[pl.ds(0, count - 1)] if many else recv.at[pl.ds(n, 1)],
                send_sem=sem.at[0],
                recv_sem=sem.at[1],
                device_id=to,
                device_id_type=MESH,
            )

        for to in targets:
            copy(to).start()
        if meanwhile:
            meanwhile()
        done = copy(targets[0], True)
        done.wait_send()
        done.wait_recv()
        parts = [recv[i] for i in range(count)]
        while len(parts) > 1:
            parts = [parts[i] + parts[i + 1] for i in range(0, len(parts), 2)]
        return parts[0]

    own_u = []
    total = sum_over(
        local, near, NEAR, asend, arecv, asem, [(row * NEAR + zc, lev) for zc in zcs[:-1]],
        lambda: own_u.append(turn(1, ubuf)),
    )
    total = sum_over(
        total, row * LEVS + lev, FAR_Y * LEVS, csend, crecv, csem,
        [
            (lax.rem(row + dy, FAR_Y) * NEAR + near, lax.rem(lev + dx, LEVS))
            for dy in (4, 3, 5, 2, 6, 1, 7, 0)
            for dx in (2, 1, 3, 0)
            if dx or dy
        ],
        lambda: turn_wait(0, own_b),
    )
    bb, bu, uu, q00, q01, q11 = [total[:, i : i + 1] for i in range(6)]

    ratio = bu / bb
    alpha0 = 1.0 / (1.0 + ratio)
    norm1 = alpha0 * alpha0 * (uu - ratio * bu)
    gb = ratio * alpha0 + norm1 / bb
    gu = -alpha0
    curve = gb * gb * (bb + q00) + 2.0 * gb * gu * (bu + q01) + gu * gu * (uu + q11)
    alpha1 = norm1 / curve
    c_b = alpha0 + alpha1 * gb
    c_u = alpha1 * gu

    for t in range(8):
        rows = slice(t * 32, t * 32 + 32)
        incr_out[0, :, t * 256 : t * 256 + 256] = c_b * bb_f[rows, :] + c_u * bu_f[rows, :]

    for copies in hops0 + hops1:
        for copy in copies:
            copy.wait_send()
    turn_wait(1, own_u[0])
    for p in range(32):
        rows = slice(p * 16, p * 16 + 16)
        control_out[0, :, p * 128 : p * 128 + 128] = c_b * ctl[0, rows, :] + c_u * ctl[1, rows, :]


def body(background_std, x_kernel, y_kernel, obs_owner, obs_cells, obs_weights, innovation, obs_precision, obs_counts):
    holding = obs_owner.shape[0]
    vmem = pl.BlockSpec(memory_space=pltpu.VMEM)
    hbm = pl.BlockSpec(memory_space=pltpu.HBM)
    field = pltpu.VMEM((256, 256), F32)
    dma = pltpu.SemaphoreType.DMA
    keep = lambda x: pltpu.with_memory_space_constraint(x, pltpu.HBM)
    return pl.pallas_call(
        kernel,
        out_shape=(
            jax.ShapeDtypeStruct((1, 16, 4096), F32),
            jax.ShapeDtypeStruct((1, 32, 2048), F32),
        ),
        in_specs=[hbm] * 9,
        out_specs=(vmem, vmem),
        scratch_shapes=[
            pltpu.VMEM((1, 32, 2048), F32), pltpu.SMEM((1, 31), F32), pltpu.SMEM((1, 31), F32),
            pltpu.VMEM((1, holding), I32), pltpu.VMEM((16, holding), I32), pltpu.VMEM((16, holding), F32),
            pltpu.VMEM((1, holding), F32), pltpu.VMEM((1, holding), F32), pltpu.SMEM((1, 1), I32),
            pltpu.VMEM((256, 128), F32), pltpu.VMEM((256, 128), F32),
            pltpu.VMEM((256, 128), F32),
            pltpu.VMEM((16, 512), F32), pltpu.VMEM((16, 512), F32), pltpu.VMEM((16, 512), F32),
            pltpu.VMEM((4, 256, 2048), BF16),
            pltpu.VMEM((1152, 256), BF16), pltpu.VMEM((1152, 256), BF16),
            pltpu.VMEM((128, 96), BF16),
            field,
            pltpu.VMEM((512, 256), BF16),
            pltpu.VMEM((512, 256), F32),
            pltpu.VMEM((2, 256, 256), F32), pltpu.VMEM((2, 256, 256), F32), pltpu.VMEM((2, 256, 256), F32),
            field, field, field, field, field,
            pltpu.VMEM((128, 128), F32), pltpu.VMEM((2, 512, 128), F32),
            pltpu.VMEM((2, 512, 128), F32), pltpu.VMEM((2, 4, 128, 128), F32),
            pltpu.VMEM((1, 1, 128), F32), pltpu.VMEM((NEAR, 1, 128), F32),
            pltpu.VMEM((1, 1, 128), F32), pltpu.VMEM((FAR_Y * LEVS, 1, 128), F32),
            dma((9,)), dma((2,)), dma((2, 2, CHUNKS)), dma((2, 2, CHUNKS)), dma((2, 2)), dma((2,)), dma((2,)), dma((3,)),
        ],
        compiler_params=pltpu.CompilerParams(
            collective_id=0, has_side_effects=True, vmem_limit_bytes=52 << 20
        ),
        name="assimilate",
    )(
        *map(keep, (background_std, x_kernel, y_kernel, obs_owner.reshape(1, holding), obs_cells.T, obs_weights.T,
        innovation.reshape(1, holding), obs_precision.reshape(1, holding))), obs_counts.reshape(1, 1),
    )


def solution(mesh):
    return jax.shard_map(
        body,
        mesh=mesh,
        in_specs=(
            P("lev", "pencil", None),
            P("lev", None),
            P("lev", None),
            P(("pencil", "lev"), None),
            P(("pencil", "lev"), None),
            P(("pencil", "lev"), None),
            P(("pencil", "lev")),
            P(("pencil", "lev")),
            P(("pencil", "lev")),
        ),
        out_specs=(P("lev", "pencil", None), P("lev", "pencil", None)),
        check_vma=False,
    )
```
